256 devices in a mesh: scen: 16 (over z, y_lo), blk: 16 (over y_hi, x, core).
Axes of the slice: x: 4, y: 4 (y_hi: 2, y_lo: 2; y = y_hi * 2 + y_lo), z: 8, core: 2. Of those that a mesh axis runs over, the one named last changes fastest.
Arguments:
- draws: bfloat16 [8192, 8192], P('blk', 'scen'), may hold values from -6 to 6
- factor: bfloat16 [8192, 8192], P('scen', 'blk'), may hold values from -0.1875 to 0.1875
- occupancy: int32 [16, 16], replicated, may hold values from 0 to 1, as said below
Outputs:
- scenarios: bfloat16 [8192, 8192], P('blk', 'scen')
The draws below stay inside these ranges and needn't reach their ends.
Inputs may be any that keep to these rules, and one draw needn't show every extreme that they name: occupancy[i, i] is 1 for every i, occupancy[i, j] is 0 for j > i, and each entry below the diagonal is 0 or 1.
All inputs are finite; a program needn't handle non-finite values.
Results may differ from the reference program's by a relative error of at most 0.001.
Values may be sent and summed in bfloat16 or wider, within the bound.
No kernel may reach another device: no remote copies, remote signals or barrier semaphores. Data moves between devices by JAX's collectives and lax.ppermute only.
A program may use at most 64 MiB of HBM per device.

```python
import jax
import jax.numpy as jnp

FACTORS = 8192
TILE = 512
SCENARIOS = 8192
TILES = 16


def draw_occupancy(key, part):
    bits = jax.random.randint(key, (TILES, TILES), 0, 2, dtype=jnp.int32)
    rows = jnp.arange(TILES, dtype=jnp.int32)[:, None]
    cols = jnp.arange(TILES, dtype=jnp.int32)[None, :]
    lower = jnp.where(cols < rows, bits, jnp.zeros_like(bits))
    return jnp.where(rows == cols, jnp.ones_like(bits), lower).astype(jnp.int32)


def steps_of(key, dims, pieces, least, largest):
    def one(axis_at, parts):
        steps = jax.random.uniform(jax.random.fold_in(jax.random.fold_in(key, 6), axis_at), (parts,), jnp.float32, least / len(pieces), largest / len(pieces))
        return jnp.repeat(jnp.exp(steps), dims[axis_at] // parts).reshape((-1,) + (1,) * (len(dims) - axis_at - 1))

    level = one(*pieces[0])
    for cut in pieces[1:]:
        level = level * one(*cut)
    return level


def gaussian(stream_key, extent, spread, most, split=(), kind=jnp.bfloat16):
    gain = steps_of(stream_key, extent, split, -0.22, 0.18) if split else 1.0
    drawn = jax.random.normal(stream_key, extent, jnp.float32) * spread * gain
    return jnp.minimum(jnp.maximum(drawn, -most), most).astype(kind)


def setup_inputs(seed: int = 0) -> dict:
    seeds = jax.random.split(jax.random.key(seed), 4)
    return {
        "draws": gaussian(seeds[0], (SCENARIOS, FACTORS), 1.0, 6.0, ((0, 16), (1, 16))),
        "factor": gaussian(seeds[1], (FACTORS, FACTORS), (2 * TILE) ** -0.5, 0.1875, ((0, 16), (1, 16))),
        "occupancy": draw_occupancy(jax.random.fold_in(seeds[3], 71), 0),
    }


def reference(draws, factor, occupancy):
    width = factor.shape[0]
    occ_full = jnp.repeat(jnp.repeat(occupancy, TILE, axis=0), TILE, axis=1)
    rows = jnp.arange(width, dtype=jnp.int32)[:, None]
    cols = jnp.arange(width, dtype=jnp.int32)[None, :]
    keep = (occ_full == 1) & (cols <= rows)
    used = jnp.where(keep, factor, jnp.zeros((), factor.dtype))
    return jnp.dot(draws, used.T, preferred_element_type=jnp.float32).astype(jnp.bfloat16)
```

```python
import functools

import jax
import jax.numpy as jnp
from jax import lax
from jax.experimental import pallas as pl
from jax.experimental.pallas import tpu as pltpu
from jax.sharding import Mesh
from jax.sharding import PartitionSpec as P

TILE = 512
HALF = TILE // 2
OFFSETS = (0, -1, 1, 2)
SWAP = [(0, 0), (1, 2), (2, 1), (3, 3)]


def shift(count, by):
    return [(i, (i + by) % count) for i in range(count)]


def y_shift(by):
    pairs = []
    for y in range(4):
        to = (y + by) % 4
        pairs.append(((y % 2) * 2 + y // 2, (to % 2) * 2 + to // 2))
    return pairs


def send_x(piece, by):
    return lax.ppermute(piece, "x", shift(4, by))


def send_y(piece, by):
    return lax.ppermute(piece, ("yl", "yh"), y_shift(by))


def gather_ring(piece, send):
    half = piece.shape[0] // 2
    before = send(piece, 1)
    after = send(piece, -1)
    return piece, before, after, send(before[:half], 1), send(after[half:], -1)


def gather_plane(tile):
    top = jnp.concatenate(gather_ring(tile[:HALF], send_x), axis=0)
    low = jnp.concatenate(gather_ring(tile[HALF:], send_y), axis=0)
    return gather_ring(top, send_y), gather_ring(low, send_x)


def kernel(meta, draws, *refs):
    tops, lows = refs[:5], refs[5:10]
    keep, send, own, other = refs[10:]
    size = keep.shape[0]
    own[...] = jnp.zeros_like(own)
    other[...] = jnp.zeros_like(other)

    def add(total, column, row_at, ref, at, piece):
        flag = meta[piece]
        begin = pl.multiple_of(meta[16 + piece] * size, size)

        def step(tile):
            total[:, column : column + HALF] += lax.dot_general(
                draws[pl.ds(begin, size), :],
                tile,
                (((1,), (1,)), ((), ())),
                preferred_element_type=jnp.float32,
            )

        @pl.when(flag == 1)
        def _():
            step(ref[pl.ds(at, HALF), :])

        @pl.when(flag == 2)
        def _():
            tile = ref[pl.ds(at, HALF), :]
            rows = row_at + lax.broadcasted_iota(jnp.int32, tile.shape, 0)
            cols = lax.broadcasted_iota(jnp.int32, tile.shape, 1)
            step(jnp.where(cols <= rows, tile, jnp.zeros_like(tile)))

    for n, (first, count) in enumerate(((0, 4), (4, 4), (8, 4), (12, 2), (14, 2))):
        total = other if n in (1, 2) else own

        def body(k, carry, total=total, ref=tops[n], first=first):
            add(total, 0, 0, ref, pl.multiple_of(k * HALF, HALF), first + k)
            return carry

        lax.fori_loop(0, count, body, 0)
    for n, (ix, iy0, count) in enumerate(
        ((0, 0, 4), (1, 0, 4), (2, 0, 4), (3, 0, 2), (3, 2, 2))
    ):
        for k in range(count):
            iy = iy0 + k
            total = other if iy in (1, 2) else own
            add(total, HALF, HALF, lows[n], k * HALF, iy * 4 + ix)

    inside = meta[32] == 1

    @pl.when(inside)
    def _():
        keep[...] = own[...]
        send[...] = other[...]

    @pl.when(jnp.logical_not(inside))
    def _():
        keep[...] = other[...]
        send[...] = own[...]


def products(meta, draws, tops, lows, size):
    out = jax.ShapeDtypeStruct((size, TILE), jnp.float32)
    vmem = pl.BlockSpec(memory_space=pltpu.VMEM)
    return pl.pallas_call(
        kernel,
        out_shape=(out, out),
        in_specs=[pl.BlockSpec(memory_space=pltpu.SMEM)] + [vmem] * 11,
        out_specs=(vmem, vmem),
        scratch_shapes=[pltpu.VMEM((size, TILE), jnp.float32)] * 2,
        compiler_params=pltpu.CompilerParams(vmem_limit_bytes=48 * 1024 * 1024),
        name="products",
    )(meta, draws, *tops, *lows)


def describe(occupancy):
    z, yl, yh, x, c = (lax.axis_index(n) for n in ("z", "yl", "yh", "x", "c"))
    off = jnp.array(OFFSETS, jnp.int32)
    y_of = ((yh * 2 + yl + off) % 4)[:, None]
    x_of = ((x + off) % 4)[None, :]
    row = 2 * z + y_of % 2 + 0 * x_of
    block = (y_of // 2) * 4 + x_of
    column = 2 * block + c
    held = occupancy[row, column] == 1
    flags = jnp.where(held & (column <= row), jnp.where(column == row, 2, 1), 0)
    inside = (yl == c).astype(jnp.int32)
    return jnp.concatenate(
        [flags.reshape(-1), block.reshape(-1), inside[None]]
    ).astype(jnp.int32)


def local(draws, factor, occupancy):
    meta = describe(occupancy)
    swapped = lax.ppermute(draws, ("yl", "c"), SWAP)
    every = lax.all_gather(swapped, "z", axis=0, tiled=True)
    tops, lows = gather_plane(factor)
    keep, send = products(meta, every, tops, lows, TILE)
    total = keep + lax.ppermute(send, "c", shift(2, 1))
    return lax.ppermute(total.astype(jnp.bfloat16), ("yl", "c"), SWAP)


def solution(mesh):
    fine = Mesh(mesh.devices.reshape(8, 2, 2, 4, 2), ("z", "yl", "yh", "x", "c"))
    scen, blk = ("z", "yl"), ("yh", "x", "c")
    return jax.shard_map(
        local,
        mesh=fine,
        in_specs=(P(blk, scen), P(scen, blk), P()),
        out_specs=P(blk, scen),
        check_vma=False,
    )
```

```python
import jax
import jax.numpy as jnp
from jax import lax
from jax.experimental import pallas as pl
from jax.experimental.pallas import tpu as pltpu
from jax.sharding import Mesh
from jax.sharding import PartitionSpec as P

TILE = 512
PARTS = 2
OFFSETS = (0, -1, 1, 2)
PLANE = ("yl", "yh", "x", "c")
SWAP = [(0, 0), (1, 2), (2, 1), (3, 3)]


def plane_id(y, x, c):
    return (((y % 2) * 2 + y // 2) * 4 + x) * 2 + c


def send(piece, by, second):
    pairs = []
    for y in range(4):
        for x in range(4):
            for c in range(2):
                along_x = (c == 0) != second
                to = (y, (x + by) % 4) if along_x else ((y + by) % 4, x)
                pairs.append((plane_id(y, x, c), plane_id(*to, c)))
    return lax.ppermute(piece, PLANE, pairs)


def kernel(meta, draws, *refs):
    pieces, (keep, give, total) = refs[:8], refs[8:]
    total[...] = jnp.zeros_like(total)
    for n, ref in enumerate(pieces):

        def body(k, carry, n=n, ref=ref):
            piece = 2 * n + k

            @pl.when(meta[piece] == 1)
            def _():
                row = meta[32 + piece]
                total[row] += jnp.dot(
                    draws[meta[16 + piece]],
                    ref[pl.ds(pl.multiple_of(k * TILE, TILE), TILE), :],
                    preferred_element_type=jnp.float32,
                )

            return carry

        lax.fori_loop(0, 2, body, 0)
    mine = meta[48]
    keep[...] = total[mine]
    give[...] = total[1 - mine]


def products(meta, draws, pieces, part):
    size = TILE // PARTS
    out = jax.ShapeDtypeStruct((size, TILE), jnp.float32)
    whole = pl.BlockSpec(memory_space=pltpu.VMEM)
    return pl.pallas_call(
        kernel,
        grid=(1,),
        out_shape=(out, out),
        in_specs=[
            pl.BlockSpec(memory_space=pltpu.SMEM),
            pl.BlockSpec((8, size, TILE), lambda i: (0, part, 0)),
        ]
        + [whole] * 8,
        out_specs=(whole, whole),
        scratch_shapes=[pltpu.VMEM((2, size, TILE), jnp.float32)],
        compiler_params=pltpu.CompilerParams(vmem_limit_bytes=40 * 1024 * 1024),
        name="products",
    )(meta, draws, *pieces)


def describe(occupancy):
    z, yl, yh, x, c = (lax.axis_index(n) for n in ("z", "yl", "yh", "x", "c"))
    off = jnp.array(OFFSETS, jnp.int32)
    outer, inner = off[:, None], off[None, :]
    x_by = jnp.where(c == 0, inner, outer)
    y_by = jnp.where(c == 0, outer, inner)
    y_of, x_of = (yh * 2 + yl + y_by) % 4, (x + x_by) % 4
    row = y_of % 2
    block = (y_of // 2) * 4 + x_of
    held = (occupancy[2 * z + row, 2 * block + c] == 1).astype(jnp.int32)
    parts = [held.reshape(-1), block.reshape(-1), row.reshape(-1), c[None]]
    return jnp.concatenate(parts).astype(jnp.int32)


def masked(factor, occupancy):
    z, yl, yh, x, c = (lax.axis_index(n) for n in ("z", "yl", "yh", "x", "c"))
    row, column = 2 * z + yl, 8 * yh + 2 * x + c
    i = row * TILE + lax.broadcasted_iota(jnp.int32, factor.shape, 0)
    j = column * TILE + lax.broadcasted_iota(jnp.int32, factor.shape, 1)
    keep = (occupancy[row, column] == 1) & (j <= i)
    return jnp.where(keep, factor, jnp.zeros((), factor.dtype)).T


def local(draws, factor, occupancy):
    meta = describe(occupancy)
    swapped = lax.ppermute(draws, ("yl", "c"), SWAP)
    tile = masked(factor, occupancy)
    before, after = send(tile, 1, False), send(tile, -1, False)
    swapped, before, after = lax.optimization_barrier((swapped, before, after))
    every = lax.all_gather(swapped, "z", axis=0)
    half = TILE // 2
    across = [send(before[:half], 1, False), send(after[half:], -1, False)]
    first = jnp.concatenate([tile, before], axis=0)
    last = jnp.concatenate([after, *across], axis=0)
    first_b, first_a = send(first, 1, True), send(first, -1, True)
    last_b, last_a = send(last, 1, True), send(last, -1, True)
    first_o, last_o = send(first_b, 1, True), send(last_a, -1, True)
    pieces = [first, last, first_b, last_b, first_a, last_a, first_o, last_o]
    sums = []
    for part in range(PARTS):
        keep, give = products(meta, every, pieces, part)
        total = keep + lax.ppermute(give, "c", [(0, 1), (1, 0)])
        sums.append(lax.ppermute(total.astype(jnp.bfloat16), ("yl", "c"), SWAP))
    return jnp.concatenate(sums, axis=0)


def solution(mesh):
    fine = Mesh(mesh.devices.reshape(8, 2, 2, 4, 2), ("z", "yl", "yh", "x", "c"))
    scen, blk = ("z", "yl"), ("yh", "x", "c")
    return jax.shard_map(
        local,
        mesh=fine,
        in_specs=(P(blk, scen), P(scen, blk), P()),
        out_specs=P(blk, scen),
        check_vma=False,
    )
```

```python
import functools

import jax
import jax.numpy as jnp
from jax import lax
from jax.experimental import pallas as pl
from jax.experimental.pallas import tpu as pltpu
from jax.sharding import Mesh
from jax.sharding import PartitionSpec as P

TILE = 512
CODED = True
PARTS = 2
EXTRA = 16
LARGEST = 32000.0
COLUMN = ("yl", "yh", "c")


def column_id(yl, yh, c):
    return (yl * 2 + yh) * 2 + c


def to_parity(tile, across):
    pairs = []
    for yl in range(2):
        for yh in range(2):
            for c in range(2):
                to = yl if c == yl else 1 - yl
                pairs.append((column_id(yl, yh, c), column_id(to, yh ^ across, c if c == yl else yl)))
    return lax.ppermute(tile, COLUMN, pairs)


def shift(name, count, piece, by):
    return lax.ppermute(piece, name, [(i, (i + by) % count) for i in range(count)])


along_x = functools.partial(shift, "x", 4)
along_z = functools.partial(shift, "z", 8)


def other_core(piece):
    return shift("c", 2, piece, 1)


def other_chip(piece):
    return shift("yl", 2, piece, 1)


def add_up(meta, draws, own, other, total, first, begin, size):
    total[...] = jnp.zeros_like(total)
    for n in range(8):
        for which, ref in ((1, own[n]), (2, other[n])):

            @pl.when(meta[first + n] == which)
            def _(n=n, ref=ref):
                total[...] += jnp.dot(
                    draws[meta[16 + n], begin : begin + size, :],
                    ref[...],
                    preferred_element_type=jnp.float32,
                )


def give_kernel(begin, size, meta, draws, *refs):
    own, other, (out, total) = refs[:8], refs[8:16], refs[16:]
    add_up(meta, draws, own, other, total, 0, begin, size)
    if not CODED:
        out[...] = total[...]
        return
    sums = total[...]
    most = jnp.max(jnp.max(jnp.abs(sums), axis=1, keepdims=True), axis=0, keepdims=True)
    power = jnp.floor(jnp.log(LARGEST / jnp.maximum(most, 1e-30)) * 1.4426950)
    out[:size, :] = jnp.round(sums * jnp.exp2(power)).astype(jnp.int32).astype(jnp.int16)
    out[size:, :] = jnp.broadcast_to(power, (EXTRA, TILE)).astype(jnp.int32).astype(jnp.int16)


def keep_kernel(begin, size, meta, draws, *refs):
    own, other, (out, total) = refs[:8], refs[8:16], refs[16:]
    add_up(meta, draws, own, other, total, 8, begin, size)
    out[...] = total[...]


def products(kernel, meta, draws, own, other, begin, size, out):
    whole = pl.BlockSpec(memory_space=pltpu.VMEM)
    return pl.pallas_call(
        functools.partial(kernel, begin, size),
        out_shape=out,
        in_specs=[pl.BlockSpec(memory_space=pltpu.SMEM)] + [whole] * 17,
        out_specs=whole,
        scratch_shapes=[pltpu.VMEM((size, TILE), jnp.float32)],
        compiler_params=pltpu.CompilerParams(vmem_limit_bytes=40 * 1024 * 1024),
        name=kernel.__name__,
    )(meta, draws, *own, *other)


def describe(occupancy):
    z, yl, yh, x, c = (lax.axis_index(n) for n in ("z", "yl", "yh", "x", "c"))
    off = jnp.array((0, 0, -1, -1, 1, 1, 2, 2), jnp.int32)
    flip = jnp.array((0, 1, 0, 1, 0, 1, 0, 1), jnp.int32)
    block = (yh ^ flip) * 4 + (x + off) % 4

    def held(row):
        where = jnp.where(row == c, 1, 2)
        return jnp.where(occupancy[2 * z + row, 2 * block + yl] == 1, where, 0)

    return jnp.concatenate([held(1 - yl), held(yl), (z - block) % 8]).astype(jnp.int32)


def masked(factor, occupancy):
    z, yl, yh, x, c = (lax.axis_index(n) for n in ("z", "yl", "yh", "x", "c"))
    row, column = 2 * z + yl, 8 * yh + 2 * x + c
    i = row * TILE + lax.broadcasted_iota(jnp.int32, factor.shape, 0)
    j = column * TILE + lax.broadcasted_iota(jnp.int32, factor.shape, 1)
    keep = (occupancy[row, column] == 1) & (j <= i)
    return jnp.where(keep, factor, jnp.zeros((), factor.dtype)).T


def local(draws, factor, occupancy):
    meta = describe(occupancy)
    tile = masked(factor, occupancy)
    near, far = to_parity(tile, 0), to_parity(tile, 1)
    up, down = [draws], [draws]
    for step in range(4):
        up.append(along_z(up[-1], 1))
        if step < 3:
            down.append(along_z(down[-1], -1))
    every = jnp.stack(up + down[:0:-1])
    near_b, far_a = along_x(near, 1), along_x(far, -1)
    far_b, near_a = along_x(far, 1), along_x(near, -1)
    near_o, far_o = along_x(near_b, 1), along_x(far_a, -1)
    own = [near, far, near_b, far_b, near_a, far_a, near_o, far_o]
    other = [other_core(piece) for piece in own]
    size = TILE // PARTS
    crossed = []
    for part in range(PARTS):
        if CODED:
            out = jax.ShapeDtypeStruct((size + EXTRA, TILE), jnp.int16)
        else:
            out = jax.ShapeDtypeStruct((size, TILE), jnp.float32)
        give = products(give_kernel, meta, every, own, other, part * size, size, out)
        crossed.append(other_chip(give))
    out = jax.ShapeDtypeStruct((TILE, TILE), jnp.float32)
    keep = products(keep_kernel, meta, every, own, other, 0, TILE, out)
    sums = []
    for part, sent in enumerate(crossed):
        if CODED:
            power = sent[size, 0].astype(jnp.float32)
            sent = sent[:size].astype(jnp.float32) * jnp.exp2(-power)
        sums.append((keep[part * size : (part + 1) * size] + sent).astype(jnp.bfloat16))
    return jnp.concatenate(sums, axis=0)


def solution(mesh):
    fine = Mesh(mesh.devices.reshape(8, 2, 2, 4, 2), ("z", "yl", "yh", "x", "c"))
    scen, blk = ("z", "yl"), ("yh", "x", "c")
    return jax.shard_map(
        local,
        mesh=fine,
        in_specs=(P(blk, scen), P(scen, blk), P()),
        out_specs=P(blk, scen),
        check_vma=False,
    )
```

```python
import functools

import jax
import jax.numpy as jnp
from jax import lax
from jax.experimental import pallas as pl
from jax.experimental.pallas import tpu as pltpu
from jax.sharding import Mesh
from jax.sharding import PartitionSpec as P

TILE = 512
PARTS = 2
SIZE = TILE // PARTS
EXTRA = 16
LARGEST = 32000.0
COLUMN = ("yl", "yh", "c")
SMEM = pl.BlockSpec(memory_space=pltpu.SMEM)
VMEM = pl.BlockSpec(memory_space=pltpu.VMEM)
PIECES = ((0, 0), (1, 0), (0, -1), (1, -1), (0, 1), (1, 1), (0, 2), (1, 2))


def column_id(yl, yh, c):
    return (yl * 2 + yh) * 2 + c


def to_parity(tile, across):
    pairs = []
    for yl in range(2):
        for yh in range(2):
            for c in range(2):
                to = yl if c == yl else 1 - yl
                pairs.append((column_id(yl, yh, c), column_id(to, yh ^ across, c if c == yl else yl)))
    return lax.ppermute(tile, COLUMN, pairs)


def shift(name, count, piece, by):
    return lax.ppermute(piece, name, [(i, (i + by) % count) for i in range(count)])


along_x = functools.partial(shift, "x", 4)
along_z = functools.partial(shift, "z", 8)


def other_core(piece):
    return shift("c", 2, piece, 1)


def other_chip(piece):
    return shift("yl", 2, piece, 1)


def call(kernel, out, scratch, specs, name):
    return pl.pallas_call(
        kernel,
        out_shape=out,
        in_specs=specs,
        out_specs=VMEM,
        scratch_shapes=scratch,
        compiler_params=pltpu.CompilerParams(vmem_limit_bytes=40 * 1024 * 1024),
        name=name,
    )


def masked_kernel(place, factor, out):
    z, yl, yh, x, c = (place[n] for n in range(5))
    ahead = (2 * z + yl - (8 * yh + 2 * x + c)) * TILE
    tile = factor[...].T
    j = lax.broadcasted_iota(jnp.int32, tile.shape, 0)
    i = lax.broadcasted_iota(jnp.int32, tile.shape, 1)
    out[...] = jnp.where(j <= i + ahead, tile, jnp.zeros_like(tile))


def masked(place, factor):
    out = jax.ShapeDtypeStruct((TILE, TILE), factor.dtype)
    return call(masked_kernel, out, [], [SMEM, VMEM], "masked")(place, factor)


def pack_kernel(*refs):
    for n, ref in enumerate(refs[:-1]):
        refs[-1][n * TILE : (n + 1) * TILE, :] = ref[...]


def pack(*tiles):
    out = jax.ShapeDtypeStruct((len(tiles) * TILE, TILE), tiles[0].dtype)
    return call(pack_kernel, out, [], [VMEM] * len(tiles), "pack")(*tiles)


def sums_kernel(given, begin, size, packs, place, occupancy, *refs):
    refs, (out, total, slots) = refs[:-3], refs[-3:]
    draws, halves, packed = refs[:7], refs[7:9], refs[9:]
    own, other = {}, {}
    for tiles, refs in ((own, packed[: len(packs[0])]), (other, packed[len(packs[0]) :])):
        for ref, pack in zip(refs, packs[tiles is other]):
            for n, piece in enumerate(pack):
                tiles[piece] = ref.at[n * TILE : (n + 1) * TILE, :]
    z, yl, yh, x, c = (place[n] for n in range(5))
    row = 1 - yl if given else yl
    for n, slot in enumerate((0, 1, 2, 3, 5, 6, 7)):
        slots[slot] = draws[n][begin : begin + size, :]
    for part in range(size // SIZE):
        slots[4, part * SIZE : (part + 1) * SIZE, :] = halves[begin // SIZE + part][...]
    total[...] = jnp.zeros_like(total)
    for n, (across, by) in enumerate(PIECES):
        block = (1 - yh if across else yh) * 4 + ((x + by) & 3)
        column = 2 * block + yl
        held = (occupancy[2 * z + row, column] == 1) & (column <= 2 * z + row)
        slot = (z - block) & 7
        for where, ref in ((row == c, own[n]), (row != c, other[n])):

            @pl.when(held & where)
            def _(slot=slot, ref=ref):
                total[...] += jnp.dot(slots[slot], ref[...], preferred_element_type=jnp.float32)

    if not given:
        out[...] = total[...]
        return
    sums = total[...].reshape(EXTRA, size // EXTRA, TILE)
    most = jnp.max(jnp.max(jnp.abs(sums), axis=1, keepdims=True), axis=2, keepdims=True)
    power = jnp.floor(jnp.log(LARGEST / jnp.maximum(most, 1e-30)) * 1.4426950)
    codes = jnp.round(sums * jnp.exp2(power)).reshape(size, TILE)
    out[:size, :] = codes.astype(jnp.int32).astype(jnp.int16)
    powers = jnp.broadcast_to(power, (EXTRA, 1, TILE)).reshape(EXTRA, TILE)
    out[size:, :] = powers.astype(jnp.int32).astype(jnp.int16)


def sums(given, begin, size, packs, out, *args):
    scratch = [pltpu.VMEM((size, TILE), jnp.float32), pltpu.VMEM((8, size, TILE), jnp.bfloat16)]
    kernel = functools.partial(sums_kernel, given, begin, size, packs)
    specs = [SMEM] * 2 + [VMEM] * (len(args) - 2)
    return call(kernel, out, scratch, specs, "give" if given else "keep")(*args)


def join_kernel(keep, *refs):
    out = refs[-1]
    for part, sent in enumerate(refs[:-1]):
        rows = slice(part * SIZE, (part + 1) * SIZE)
        power = sent[SIZE:, :].astype(jnp.int32).astype(jnp.float32).reshape(EXTRA, 1, TILE)
        codes = sent[:SIZE, :].astype(jnp.int32).astype(jnp.float32).reshape(EXTRA, SIZE // EXTRA, TILE)
        crossed = (codes * jnp.exp2(-power)).reshape(SIZE, TILE)
        out[rows, :] = (keep[rows, :] + crossed).astype(out.dtype)


def join(keep, crossed):
    out = jax.ShapeDtypeStruct((TILE, TILE), jnp.bfloat16)
    return call(join_kernel, out, [], [VMEM] * (1 + PARTS), "join")(keep, *crossed)


def local(draws, factor, occupancy):
    place = jnp.stack([lax.axis_index(n) for n in ("z", "yl", "yh", "x", "c")]).astype(jnp.int32)
    together = lax.optimization_barrier
    tile = masked(place, factor)
    near, far = to_parity(tile, 0), to_parity(tile, 1)
    up1, down1 = along_z(draws, 1), along_z(draws, -1)
    up1, down1, near, far = together((up1, down1, near, far))
    pair = pack(near, far)
    up2, down2 = along_z(up1, 1), along_z(down1, -1)
    before, after = along_x(pair, 1), along_x(pair, -1)
    pair_c = other_core(pair)
    up2, down2, pair_c = together((up2, down2, pair_c))
    up3, down3 = along_z(up2, 1), along_z(down2, -1)
    near_o, far_o = along_x(before[:TILE], 1), along_x(after[TILE:], -1)
    up3, down3, before, after = together((up3, down3, before, after))
    up4, down4 = along_z(up3[:SIZE], 1), along_z(down3[SIZE:], -1)
    before_c, after_c = other_core(before), other_core(after)
    up4, down4, near_o, far_o = together((up4, down4, near_o, far_o))
    last_c = other_core(pack(near_o, far_o))
    packs = ((0, 1), (2, 3), (4, 5), (6,), (7,)), ((0, 1), (2, 3), (4, 5), (6, 7))
    args = (place, occupancy, draws, up1, up2, up3, down3, down2, down1, up4, down4)
    args += (pair, before, after, near_o, far_o, pair_c, before_c, after_c, last_c)
    coded = jax.ShapeDtypeStruct((SIZE + EXTRA, TILE), jnp.int16)
    crossed = [other_chip(sums(True, part * SIZE, SIZE, packs, coded, *args)) for part in range(PARTS)]
    keep = sums(False, 0, TILE, packs, jax.ShapeDtypeStruct((TILE, TILE), jnp.float32), *args)
    return join(keep, crossed)


def solution(mesh):
    fine = Mesh(mesh.devices.reshape(8, 2, 2, 4, 2), ("z", "yl", "yh", "x", "c"))
    scen, blk = ("z", "yl"), ("yh", "x", "c")
    return jax.shard_map(
        local,
        mesh=fine,
        in_specs=(P(blk, scen), P(scen, blk), P()),
        out_specs=P(blk, scen),
        check_vma=False,
    )
```

```python
import functools

import jax
import jax.numpy as jnp
from jax import lax
from jax.experimental import pallas as pl
from jax.experimental.pallas import tpu as pltpu
from jax.sharding import Mesh
from jax.sharding import PartitionSpec as P

TILE = 512
HALF = TILE // 2
PARTS = ((0, 128), (128, 384))
EXTRA = 16
LARGEST = 32000.0
COLUMN = ("yl", "yh", "c")
SMEM = pl.BlockSpec(memory_space=pltpu.SMEM)
VMEM = pl.BlockSpec(memory_space=pltpu.VMEM)
PIECES = ((0, 0), (1, 0), (0, -1), (1, -1), (0, 1), (1, 1), (0, 2), (1, 2))


def column_id(yl, yh, c):
    return (yl * 2 + yh) * 2 + c


def to_parity(tile, across):
    pairs = []
    for yl in range(2):
        for yh in range(2):
            for c in range(2):
                to = yl if c == yl else 1 - yl
                pairs.append((column_id(yl, yh, c), column_id(to, yh ^ across, c if c == yl else yl)))
    return lax.ppermute(tile, COLUMN, pairs)


def shift(name, count, piece, by):
    return lax.ppermute(piece, name, [(i, (i + by) % count) for i in range(count)])


along_x = functools.partial(shift, "x", 4)
along_z = functools.partial(shift, "z", 8)


def other_core(piece):
    return shift("c", 2, piece, 1)


def other_chip(piece):
    return shift("yl", 2, piece, 1)


def call(kernel, out, scratch, specs, name, out_specs=VMEM):
    return pl.pallas_call(
        kernel,
        out_shape=out,
        in_specs=specs,
        out_specs=out_specs,
        scratch_shapes=scratch,
        compiler_params=pltpu.CompilerParams(vmem_limit_bytes=40 * 1024 * 1024),
        name=name,
    )


def masked_kernel(place, factor, out):
    z, yl, yh, x, c = (place[n] for n in range(5))
    ahead = (2 * z + yl - (8 * yh + 2 * x + c)) * TILE
    tile = factor[...].T
    j = lax.broadcasted_iota(jnp.int32, tile.shape, 0)
    i = lax.broadcasted_iota(jnp.int32, tile.shape, 1)
    out[...] = jnp.where(j <= i + ahead, tile, jnp.zeros_like(tile))


def masked(place, factor):
    out = jax.ShapeDtypeStruct((TILE, TILE), factor.dtype)
    return call(masked_kernel, out, [], [SMEM, VMEM], "masked")(place, factor)


def pack_kernel(*refs):
    at = 0
    for ref in refs[:-1]:
        refs[-1][at : at + ref.shape[0], :] = ref[...]
        at += ref.shape[0]


def pack(*tiles):
    out = jax.ShapeDtypeStruct((sum(tile.shape[0] for tile in tiles), TILE), tiles[0].dtype)
    return call(pack_kernel, out, [], [VMEM] * len(tiles), "pack")(*tiles)


def add_up(row, ready, begin, size, packs, place, occupancy, draws, halves, packed, total, slots):
    own, other = {}, {}
    for tiles, refs in ((own, packed[: len(packs[0])]), (other, packed[len(packs[0]) :])):
        for ref, pack in zip(refs, packs[tiles is other]):
            for n, piece in enumerate(pack):
                tiles[piece] = ref.at[n * TILE : (n + 1) * TILE, :]
    z, yl, yh, x, c = (place[n] for n in range(5))
    for n, slot in enumerate((0, 1, 2, 3, 5, 6, 7)):
        slots[slot] = draws[n][begin : begin + size, :]
    for n, half in enumerate(halves):
        low, high = max(begin, n * HALF), min(begin + size, (n + 1) * HALF)
        if low < high:
            slots[4, low - begin : high - begin, :] = half[low - n * HALF : high - n * HALF, :]
    for n, (across, by) in enumerate(PIECES[:6] if ready else PIECES):
        block = (1 - yh if across else yh) * 4 + ((x + by) & 3)
        column = 2 * block + yl
        slot = (z - block) & 7
        held = (occupancy[2 * z + row, column] == 1) & (column <= 2 * z + row)
        if ready:
            held &= slot != 4
        elif n < 6:
            held &= slot == 4
        for where, ref in ((row == c, own[n]), (row != c, other[n])):

            @pl.when(held & where)
            def _(slot=slot, ref=ref):
                total[...] += jnp.dot(slots[slot], ref[...], preferred_element_type=jnp.float32)


def early_kernel(packs, place, occupancy, *refs):
    draws, packed, (give, keep, slots) = refs[:7], refs[7:-3], refs[-3:]
    for row, total in ((1 - place[1], give), (place[1], keep)):
        total[...] = jnp.zeros_like(total)
        add_up(row, True, 0, TILE, packs, place, occupancy, draws, (), packed, total, slots)


def early(packs, *args):
    out = jax.ShapeDtypeStruct((TILE, TILE), jnp.float32)
    specs = [SMEM] * 2 + [VMEM] * (len(args) - 2)
    scratch = [pltpu.VMEM((8, TILE, TILE), jnp.bfloat16)]
    kernel = functools.partial(early_kernel, packs)
    return call(kernel, (out, out), scratch, specs, "early", (VMEM, VMEM))(*args)


def late_kernel(given, begin, size, packs, place, occupancy, so_far, *refs):
    draws, halves, packed, (out, total, slots) = refs[:7], refs[7:9], refs[9:-3], refs[-3:]
    total[...] = so_far[begin : begin + size, :]
    row = 1 - place[1] if given else place[1]
    add_up(row, False, begin, size, packs, place, occupancy, draws, halves, packed, total, slots)
    if not given:
        out[...] = total[...]
        return
    sums = total[...].reshape(EXTRA, size // EXTRA, TILE)
    most = jnp.max(jnp.max(jnp.abs(sums), axis=1, keepdims=True), axis=2, keepdims=True)
    power = jnp.floor(jnp.log(LARGEST / jnp.maximum(most, 1e-30)) * 1.4426950)
    codes = jnp.round(sums * jnp.exp2(power)).reshape(size, TILE)
    out[:size, :] = codes.astype(jnp.int32).astype(jnp.int16)
    powers = jnp.broadcast_to(power, (EXTRA, 1, TILE)).reshape(EXTRA, TILE)
    out[size:, :] = powers.astype(jnp.int32).astype(jnp.int16)


def late(given, begin, size, packs, out, *args):
    scratch = [pltpu.VMEM((size, TILE), jnp.float32), pltpu.VMEM((8, size, TILE), jnp.bfloat16)]
    kernel = functools.partial(late_kernel, given, begin, size, packs)
    specs = [SMEM] * 2 + [VMEM] * (len(args) - 2)
    return call(kernel, out, scratch, specs, "give" if given else "keep")(*args)


def join_kernel(keep, *refs):
    out = refs[-1]
    for sent, (begin, size) in zip(refs, PARTS):
        rows = slice(begin, begin + size)
        power = sent[size:, :].astype(jnp.int32).astype(jnp.float32).reshape(EXTRA, 1, TILE)
        codes = sent[:size, :].astype(jnp.int32).astype(jnp.float32).reshape(EXTRA, size // EXTRA, TILE)
        crossed = (codes * jnp.exp2(-power)).reshape(size, TILE)
        out[rows, :] = (keep[rows, :] + crossed).astype(out.dtype)


def join(keep, crossed):
    out = jax.ShapeDtypeStruct((TILE, TILE), jnp.bfloat16)
    return call(join_kernel, out, [], [VMEM] * (1 + len(crossed)), "join")(keep, *crossed)


def local(draws, factor, occupancy):
    place = jnp.stack([lax.axis_index(n) for n in ("z", "yl", "yh", "x", "c")]).astype(jnp.int32)
    together = lax.optimization_barrier
    tile = masked(place, factor)
    near, far = to_parity(tile, 0), to_parity(tile, 1)
    up1, down1 = along_z(draws, 1), along_z(draws, -1)
    up1, down1, near, far = together((up1, down1, near, far))
    pair = pack(near, far)
    up2, down2 = along_z(up1, 1), along_z(down1, -1)
    before, after = along_x(pair, 1), along_x(pair, -1)
    up2, down2 = together((up2, down2))
    up3, down3 = along_z(up2, 1), along_z(down2, -1)
    near_o, far_o = along_x(before[:TILE], 1), along_x(after[TILE:], -1)
    up3, down3, before, after = together((up3, down3, before, after))
    up4, down4 = along_z(up3[:HALF], 1), along_z(down3[HALF:], -1)
    pair_c, before_c, after_c = other_core(pair), other_core(before), other_core(after)
    up4, down4, near_o, far_o = together((up4, down4, near_o, far_o))
    last_c = other_core(pack(near_o, far_o))
    circled = (draws, up1, up2, up3, down3, down2, down1)
    ready = ((0, 1), (2, 3), (4, 5))
    give, keep = early((ready, ready), place, occupancy, *circled, pair, before, after, pair_c, before_c, after_c)
    packs = ready + ((6,), (7,)), ready + ((6, 7),)
    args = (*circled, up4, down4, pair, before, after, near_o, far_o, pair_c, before_c, after_c, last_c)
    crossed = []
    for begin, size in PARTS:
        coded = jax.ShapeDtypeStruct((size + EXTRA, TILE), jnp.int16)
        crossed.append(other_chip(late(True, begin, size, packs, coded, place, occupancy, give, *args)))
    keep = late(False, 0, TILE, packs, jax.ShapeDtypeStruct((TILE, TILE), jnp.float32), place, occupancy, keep, *args)
    return join(keep, crossed)


def solution(mesh):
    fine = Mesh(mesh.devices.reshape(8, 2, 2, 4, 2), ("z", "yl", "yh", "x", "c"))
    scen, blk = ("z", "yl"), ("yh", "x", "c")
    return jax.shard_map(
        local,
        mesh=fine,
        in_specs=(P(blk, scen), P(scen, blk), P()),
        out_specs=P(blk, scen),
        check_vma=False,
    )
```

```python
import functools

import jax
import jax.numpy as jnp
from jax import lax
from jax.experimental import pallas as pl
from jax.experimental.pallas import tpu as pltpu
from jax.sharding import Mesh
from jax.sharding import PartitionSpec as P

TILE = 512
HALF = TILE // 2
PARTS = ((0, 128), (128, 384))
EXTRA = 16
LARGEST = 32000.0
COLUMN = ("yl", "yh", "c")
SMEM = pl.BlockSpec(memory_space=pltpu.SMEM)
VMEM = pl.BlockSpec(memory_space=pltpu.VMEM)
PIECES = ((0, 0), (1, 0), (0, -1), (1, -1), (0, 1), (1, 1), (0, 2), (1, 2))


def column_id(yl, yh, c):
    return (yl * 2 + yh) * 2 + c


def to_parity(tile, across):
    pairs = []
    for yl in range(2):
        for yh in range(2):
            for c in range(2):
                to = yl if c == yl else 1 - yl
                pairs.append((column_id(yl, yh, c), column_id(to, yh ^ across, c if c == yl else yl)))
    return lax.ppermute(tile, COLUMN, pairs)


def shift(name, count, piece, by):
    return lax.ppermute(piece, name, [(i, (i + by) % count) for i in range(count)])


along_x = functools.partial(shift, "x", 4)
along_z = functools.partial(shift, "z", 8)


def other_core(piece):
    return shift("c", 2, piece, 1)


def other_chip(piece):
    return shift("yl", 2, piece, 1)


def call(kernel, out, scratch, specs, name, out_specs=VMEM):
    return pl.pallas_call(
        kernel,
        out_shape=out,
        in_specs=specs,
        out_specs=out_specs,
        scratch_shapes=scratch,
        compiler_params=pltpu.CompilerParams(vmem_limit_bytes=40 * 1024 * 1024),
        name=name,
    )


def masked_kernel(place, factor, out):
    z, yl, yh, x, c = (place[n] for n in range(5))
    ahead = (2 * z + yl - (8 * yh + 2 * x + c)) * TILE
    tile = factor[...].T
    j = lax.broadcasted_iota(jnp.int32, tile.shape, 0)
    i = lax.broadcasted_iota(jnp.int32, tile.shape, 1)
    out[...] = jnp.where(j <= i + ahead, tile, jnp.zeros_like(tile))


def masked(place, factor):
    out = jax.ShapeDtypeStruct((TILE, TILE), factor.dtype)
    return call(masked_kernel, out, [], [SMEM, VMEM], "masked")(place, factor)


def pack_kernel(*refs):
    at = 0
    for ref in refs[:-1]:
        refs[-1][at : at + ref.shape[0], :] = ref[...]
        at += ref.shape[0]


def pack(*tiles):
    out = jax.ShapeDtypeStruct((sum(tile.shape[0] for tile in tiles), TILE), tiles[0].dtype)
    return call(pack_kernel, out, [], [VMEM] * len(tiles), "pack")(*tiles)


def add_up(row, ready, begin, size, packs, place, occupancy, draws, halves, packed, total, slots):
    own, other = {}, {}
    for tiles, refs in ((own, packed[: len(packs[0])]), (other, packed[len(packs[0]) :])):
        for ref, pack in zip(refs, packs[tiles is other]):
            for n, piece in enumerate(pack):
                tiles[piece] = ref.at[n * TILE : (n + 1) * TILE, :]
    z, yl, yh, x, c = (place[n] for n in range(5))
    for n, slot in enumerate((0, 1, 2, 3, 5, 6, 7)):
        slots[slot] = draws[n][begin : begin + size, :]
    for n, half in enumerate(halves):
        low, high = max(begin, n * HALF), min(begin + size, (n + 1) * HALF)
        if low < high:
            slots[4, low - begin : high - begin, :] = half[low - n * HALF : high - n * HALF, :]
    for n, (across, by) in enumerate(PIECES[:6] if ready else PIECES):
        block = (1 - yh if across else yh) * 4 + ((x + by) & 3)
        column = 2 * block + yl
        slot = (z - block) & 7
        held = (occupancy[2 * z + row, column] == 1) & (column <= 2 * z + row)
        if ready:
            held &= slot != 4
        elif n < 6:
            held &= slot == 4
        for where, ref in ((row == c, own[n]), (row != c, other[n])):

            @pl.when(held & where)
            def _(slot=slot, ref=ref):
                total[...] += jnp.dot(slots[slot], ref[...], preferred_element_type=jnp.float32)


def early_kernel(packs, place, occupancy, *refs):
    draws, packed, (give, keep, slots) = refs[:7], refs[7:-3], refs[-3:]
    for row, total in ((1 - place[1], give), (place[1], keep)):
        total[...] = jnp.zeros_like(total)
        add_up(row, True, 0, TILE, packs, place, occupancy, draws, (), packed, total, slots)


def early(packs, *args):
    out = jax.ShapeDtypeStruct((TILE, TILE), jnp.float32)
    specs = [SMEM] * 2 + [VMEM] * (len(args) - 2)
    scratch = [pltpu.VMEM((8, TILE, TILE), jnp.bfloat16)]
    kernel = functools.partial(early_kernel, packs)
    return call(kernel, (out, out), scratch, specs, "early", (VMEM, VMEM))(*args)


def late_kernel(given, begin, size, packs, place, occupancy, so_far, *refs):
    draws, halves, packed, (out, total, slots) = refs[:7], refs[7:9], refs[9:-3], refs[-3:]
    total[...] = so_far[begin : begin + size, :]
    row = 1 - place[1] if given else place[1]
    add_up(row, False, begin, size, packs, place, occupancy, draws, halves, packed, total, slots)
    if not given:
        out[...] = total[...]
        return
    sums = total[...].reshape(EXTRA, size // EXTRA, TILE)
    most = jnp.max(jnp.max(jnp.abs(sums), axis=1, keepdims=True), axis=2, keepdims=True)
    power = jnp.floor(jnp.log(LARGEST / jnp.maximum(most, 1e-30)) * 1.4426950)
    codes = jnp.round(sums * jnp.exp2(power)).reshape(size, TILE)
    out[:size, :] = codes.astype(jnp.int32).astype(jnp.int16)
    powers = jnp.broadcast_to(power, (EXTRA, 1, TILE)).reshape(EXTRA, TILE)
    out[size:, :] = powers.astype(jnp.int32).astype(jnp.int16)


def late(given, begin, size, packs, out, *args):
    scratch = [pltpu.VMEM((size, TILE), jnp.float32), pltpu.VMEM((8, size, TILE), jnp.bfloat16)]
    kernel = functools.partial(late_kernel, given, begin, size, packs)
    specs = [SMEM] * 2 + [VMEM] * (len(args) - 2)
    return call(kernel, out, scratch, specs, "give" if given else "keep")(*args)


def join_kernel(keep, *refs):
    out = refs[-1]
    for sent, (begin, size) in zip(refs, PARTS):
        rows = slice(begin, begin + size)
        power = sent[size:, :].astype(jnp.int32).astype(jnp.float32).reshape(EXTRA, 1, TILE)
        codes = sent[:size, :].astype(jnp.int32).astype(jnp.float32).reshape(EXTRA, size // EXTRA, TILE)
        crossed = (codes * jnp.exp2(-power)).reshape(size, TILE)
        out[rows, :] = (keep[rows, :] + crossed).astype(out.dtype)


def join(keep, crossed):
    out = jax.ShapeDtypeStruct((TILE, TILE), jnp.bfloat16)
    return call(join_kernel, out, [], [VMEM] * (1 + len(crossed)), "join")(keep, *crossed)


def local(draws, factor, occupancy):
    place = jnp.stack([lax.axis_index(n) for n in ("z", "yl", "yh", "x", "c")]).astype(jnp.int32)
    together = lax.optimization_barrier
    up1, down1 = along_z(draws, 1), along_z(draws, -1)
    up1, down1 = together((up1, down1))
    tile = masked(place, factor)
    far, near = to_parity(tile, 1), to_parity(tile, 0)
    pair = pack(near, far)
    up2, down2 = along_z(up1, 1), along_z(down1, -1)
    before, after = along_x(pair, 1), along_x(pair, -1)
    up2, down2 = together((up2, down2))
    up3, down3 = along_z(up2, 1), along_z(down2, -1)
    near_o, far_o = along_x(before[:TILE], 1), along_x(after[TILE:], -1)
    up3, down3, before, after = together((up3, down3, before, after))
    up4, down4 = along_z(up3[:HALF], 1), along_z(down3[HALF:], -1)
    pair_c, before_c, after_c = other_core(pair), other_core(before), other_core(after)
    up4, down4, near_o, far_o = together((up4, down4, near_o, far_o))
    last_c = other_core(pack(near_o, far_o))
    circled = (draws, up1, up2, up3, down3, down2, down1)
    ready = ((0, 1), (2, 3), (4, 5))
    give, keep = early((ready, ready), place, occupancy, *circled, pair, before, after, pair_c, before_c, after_c)
    packs = ready + ((6,), (7,)), ready + ((6, 7),)
    args = (*circled, up4, down4, pair, before, after, near_o, far_o, pair_c, before_c, after_c, last_c)
    crossed = []
    for begin, size in PARTS:
        coded = jax.ShapeDtypeStruct((size + EXTRA, TILE), jnp.int16)
        crossed.append(other_chip(late(True, begin, size, packs, coded, place, occupancy, give, *args)))
    keep = late(False, 0, TILE, packs, jax.ShapeDtypeStruct((TILE, TILE), jnp.float32), place, occupancy, keep, *args)
    return join(keep, crossed)


def solution(mesh):
    fine = Mesh(mesh.devices.reshape(8, 2, 2, 4, 2), ("z", "yl", "yh", "x", "c"))
    scen, blk = ("z", "yl"), ("yh", "x", "c")
    return jax.shard_map(
        local,
        mesh=fine,
        in_specs=(P(blk, scen), P(scen, blk), P()),
        out_specs=P(blk, scen),
        check_vma=False,
    )
```

```python
import functools

import jax
import jax.numpy as jnp
from jax import lax
from jax.experimental import pallas as pl
from jax.experimental.pallas import tpu as pltpu
from jax.sharding import Mesh
from jax.sharding import PartitionSpec as P

TILE = 512
HALF = TILE // 2
PARTS = ((0, 128), (128, 384))
EXTRA = 16
LARGEST = 32000.0
COLUMN = ("yl", "yh", "c")
SMEM = pl.BlockSpec(memory_space=pltpu.SMEM)
VMEM = pl.BlockSpec(memory_space=pltpu.VMEM)
PIECES = ((0, 0), (1, 0), (0, -1), (1, -1), (0, 1), (1, 1), (0, 2), (1, 2))


def column_id(yl, yh, c):
    return (yl * 2 + yh) * 2 + c


def to_parity(tile, across):
    pairs = []
    for yl in range(2):
        for yh in range(2):
            for c in range(2):
                to = yl if c == yl else 1 - yl
                pairs.append((column_id(yl, yh, c), column_id(to, yh ^ across, c if c == yl else yl)))
    return lax.ppermute(tile, COLUMN, pairs)


def shift(name, count, piece, by):
    return lax.ppermute(piece, name, [(i, (i + by) % count) for i in range(count)])


along_x = functools.partial(shift, "x", 4)
along_z = functools.partial(shift, "z", 8)


def other_core(piece):
    return shift("c", 2, piece, 1)


def other_chip(piece):
    return shift("yl", 2, piece, 1)


def call(kernel, out, scratch, specs, name, out_specs=VMEM):
    return pl.pallas_call(
        kernel,
        out_shape=out,
        in_specs=specs,
        out_specs=out_specs,
        scratch_shapes=scratch,
        compiler_params=pltpu.CompilerParams(vmem_limit_bytes=40 * 1024 * 1024),
        name=name,
    )


def masked_kernel(place, factor, out):
    z, yl, yh, x, c = (place[n] for n in range(5))
    ahead = (2 * z + yl - (8 * yh + 2 * x + c)) * TILE
    tile = factor[...].T
    j = lax.broadcasted_iota(jnp.int32, tile.shape, 0)
    i = lax.broadcasted_iota(jnp.int32, tile.shape, 1)
    out[...] = jnp.where(j <= i + ahead, tile, jnp.zeros_like(tile))


def masked(place, factor):
    out = jax.ShapeDtypeStruct((TILE, TILE), factor.dtype)
    return call(masked_kernel, out, [], [SMEM, VMEM], "masked")(place, factor)


def pack_kernel(*refs):
    at = 0
    for ref in refs[:-1]:
        refs[-1][at : at + ref.shape[0], :] = ref[...]
        at += ref.shape[0]


def pack(*tiles):
    out = jax.ShapeDtypeStruct((sum(tile.shape[0] for tile in tiles), TILE), tiles[0].dtype)
    return call(pack_kernel, out, [], [VMEM] * len(tiles), "pack")(*tiles)


def add_up(row, ready, begin, size, packs, place, occupancy, draws, halves, packed, total, slots):
    own, other = {}, {}
    for tiles, refs in ((own, packed[: len(packs[0])]), (other, packed[len(packs[0]) :])):
        for ref, pack in zip(refs, packs[tiles is other]):
            for n, piece in enumerate(pack):
                tiles[piece] = ref.at[n * TILE : (n + 1) * TILE, :]
    z, yl, yh, x, c = (place[n] for n in range(5))
    for n, slot in enumerate((0, 1, 2, 3, 5, 6, 7)):
        slots[slot] = draws[n][begin : begin + size, :]
    for n, half in enumerate(halves):
        low, high = max(begin, n * HALF), min(begin + size, (n + 1) * HALF)
        if low < high:
            slots[4, low - begin : high - begin, :] = half[low - n * HALF : high - n * HALF, :]
    for n, (across, by) in enumerate(PIECES[:6] if ready else PIECES):
        block = (1 - yh if across else yh) * 4 + ((x + by) & 3)
        column = 2 * block + yl
        slot = (z - block) & 7
        held = (occupancy[2 * z + row, column] == 1) & (column <= 2 * z + row)
        if ready:
            held &= slot != 4
        elif ready is False and n < 6:
            held &= slot == 4
        for where, ref in ((row == c, own[n]), (row != c, other[n])):

            @pl.when(held & where)
            def _(slot=slot, ref=ref):
                total[...] += jnp.dot(slots[slot], ref[...], preferred_element_type=jnp.float32)


def early_kernel(packs, place, occupancy, *refs):
    draws, packed, (give, slots) = refs[:7], refs[7:-2], refs[-2:]
    give[...] = jnp.zeros_like(give)
    add_up(1 - place[1], True, 0, TILE, packs, place, occupancy, draws, (), packed, give, slots)


def early(packs, *args):
    out = jax.ShapeDtypeStruct((TILE, TILE), jnp.float32)
    specs = [SMEM] * 2 + [VMEM] * (len(args) - 2)
    scratch = [pltpu.VMEM((8, TILE, TILE), jnp.bfloat16)]
    kernel = functools.partial(early_kernel, packs)
    return call(kernel, out, scratch, specs, "early")(*args)


def late_kernel(given, begin, size, packs, place, occupancy, *refs):
    if given:
        so_far, refs = refs[0], refs[1:]
    draws, halves, packed, (out, total, slots) = refs[:7], refs[7:9], refs[9:-3], refs[-3:]
    total[...] = so_far[begin : begin + size, :] if given else jnp.zeros_like(total)
    row = 1 - place[1] if given else place[1]
    add_up(row, False if given else None, begin, size, packs, place, occupancy, draws, halves, packed, total, slots)
    if not given:
        out[...] = total[...]
        return
    sums = total[...].reshape(EXTRA, size // EXTRA, TILE)
    most = jnp.max(jnp.max(jnp.abs(sums), axis=1, keepdims=True), axis=2, keepdims=True)
    power = jnp.floor(jnp.log(LARGEST / jnp.maximum(most, 1e-30)) * 1.4426950)
    codes = jnp.round(sums * jnp.exp2(power)).reshape(size, TILE)
    out[:size, :] = codes.astype(jnp.int32).astype(jnp.int16)
    powers = jnp.broadcast_to(power, (EXTRA, 1, TILE)).reshape(EXTRA, TILE)
    out[size:, :] = powers.astype(jnp.int32).astype(jnp.int16)


def late(given, begin, size, packs, out, *args):
    scratch = [pltpu.VMEM((size, TILE), jnp.float32), pltpu.VMEM((8, size, TILE), jnp.bfloat16)]
    kernel = functools.partial(late_kernel, given, begin, size, packs)
    specs = [SMEM] * 2 + [VMEM] * (len(args) - 2)
    return call(kernel, out, scratch, specs, "give" if given else "keep")(*args)


def join_kernel(keep, *refs):
    out = refs[-1]
    for sent, (begin, size) in zip(refs, PARTS):
        rows = slice(begin, begin + size)
        power = sent[size:, :].astype(jnp.int32).astype(jnp.float32).reshape(EXTRA, 1, TILE)
        codes = sent[:size, :].astype(jnp.int32).astype(jnp.float32).reshape(EXTRA, size // EXTRA, TILE)
        crossed = (codes * jnp.exp2(-power)).reshape(size, TILE)
        out[rows, :] = (keep[rows, :] + crossed).astype(out.dtype)


def join(keep, crossed):
    out = jax.ShapeDtypeStruct((TILE, TILE), jnp.bfloat16)
    return call(join_kernel, out, [], [VMEM] * (1 + len(crossed)), "join")(keep, *crossed)


def local(draws, factor, occupancy):
    place = jnp.stack([lax.axis_index(n) for n in ("z", "yl", "yh", "x", "c")]).astype(jnp.int32)
    together = lax.optimization_barrier
    up1, down1 = along_z(draws, 1), along_z(draws, -1)
    up1, down1 = together((up1, down1))
    tile = masked(place, factor)
    far, near = to_parity(tile, 1), to_parity(tile, 0)
    pair = pack(near, far)
    up2, down2 = along_z(up1, 1), along_z(down1, -1)
    before, after = along_x(pair, 1), along_x(pair, -1)
    up2, down2 = together((up2, down2))
    up3, down3 = along_z(up2, 1), along_z(down2, -1)
    near_o, far_o = along_x(before[:TILE], 1), along_x(after[TILE:], -1)
    up3, down3, before, after = together((up3, down3, before, after))
    up4, down4 = along_z(up3[:HALF], 1), along_z(down3[HALF:], -1)
    pair_c, before_c, after_c = other_core(pair), other_core(before), other_core(after)
    up4, down4, near_o, far_o = together((up4, down4, near_o, far_o))
    last_c = other_core(pack(near_o, far_o))
    circled = (draws, up1, up2, up3, down3, down2, down1)
    ready = ((0, 1), (2, 3), (4, 5))
    give = early((ready, ready), place, occupancy, *circled, pair, before, after, pair_c, before_c, after_c)
    packs = ready + ((6,), (7,)), ready + ((6, 7),)
    args = (*circled, up4, down4, pair, before, after, near_o, far_o, pair_c, before_c, after_c, last_c)
    crossed = []
    for begin, size in PARTS:
        coded = jax.ShapeDtypeStruct((size + EXTRA, TILE), jnp.int16)
        crossed.append(other_chip(late(True, begin, size, packs, coded, place, occupancy, give, *args)))
    keep = late(False, 0, TILE, packs, jax.ShapeDtypeStruct((TILE, TILE), jnp.float32), place, occupancy, *args)
    return join(keep, crossed)


def solution(mesh):
    fine = Mesh(mesh.devices.reshape(8, 2, 2, 4, 2), ("z", "yl", "yh", "x", "c"))
    scen, blk = ("z", "yl"), ("yh", "x", "c")
    return jax.shard_map(
        local,
        mesh=fine,
        in_specs=(P(blk, scen), P(scen, blk), P()),
        out_specs=P(blk, scen),
        check_vma=False,
    )
```
